256 devices in a mesh: vessel: 2 (over core), gather: 128 (over y, x, z).
Axes of the slice: x: 4, y: 4, z: 8, core: 2. Of those that a mesh axis runs over, the one named last changes fastest.
Arguments:
- observed: bfloat16 [128, 128, 2048], P('gather'), may hold values from -6 to 6
- estimate: bfloat16 [2, 128, 128, 2048], P('vessel', 'gather'), may hold values from -6 to 6
- delays: int32 [2, 128], P('vessel', 'gather'), may hold values from 0 to 256
- taps_time: float32 [16, 7], replicated, may hold values from -2 to 2
- taps_shot: float32 [16, 7], replicated, may hold values from -0.5 to 0.5
- thresh: float32 [16], replicated, may hold values from 0.02 to 0.3
Outputs:
- deblended: bfloat16 [2, 128, 128, 2048], P('vessel', 'gather')
The draws below stay inside these ranges and needn't reach their ends.
All inputs are finite; a program needn't handle non-finite values.
Results may differ from the reference program's by a relative error of at most 0.022.
Values may be sent and summed in bfloat16 or wider, within the bound.
No kernel may reach another device: no remote copies, remote signals or barrier semaphores. Data moves between devices by JAX's collectives and lax.ppermute only.
A program may use at most 64 MiB of HBM per device.

```python
import math
import jax
import jax.numpy as jnp
from jax import lax

TT = 2048
CH = 16
TAPS = 7
TIME_SPACING = 4
SHOT_SPACING = 2
MAXD = 256
ITERS = 2
VES = 2
SHOTS = 128
REC = 128


def with_ends(array, rng, least, largest):
    extent = array.shape
    spot = [jax.random.randint(jax.random.fold_in(rng, axis), (), 0, extent[axis]) for axis in range(len(extent))]
    array = array.at[tuple(spot)].set(least)
    longest = extent.index(max(extent))
    spot[longest] = (spot[longest] + 1) % extent[longest]
    return array.at[tuple(spot)].set(largest)


def block_scale(key, shape, shards, smallest, largest):
    gain = 1.0
    for axis_at, blocks in shards:
        draws = jax.random.uniform(jax.random.fold_in(jax.random.fold_in(key, 6), axis_at), (blocks,), jnp.float32, smallest / len(shards), largest / len(shards))
        gain = gain * jnp.repeat(jnp.exp(draws), shape[axis_at] // blocks).reshape((-1,) + (1,) * (len(shape) - 1 - axis_at))
    return gain


def scatter_about(stream_key, dims, deviation, most, shards=(), held_as=jnp.bfloat16):
    loudness = block_scale(stream_key, dims, shards, -0.22, 0.18) if shards else 1.0
    result = jax.random.normal(stream_key, dims, jnp.float32) * deviation * loudness
    return jnp.minimum(jnp.maximum(result, -most), most).astype(held_as)


def setup_inputs(seed: int = 0) -> dict:
    keys = jax.random.split(jax.random.key(seed), 7)
    observed = scatter_about(keys[0], (SHOTS, REC, TT), 1.0, 6.0, ((0, 128),))
    estimate = scatter_about(keys[1], (VES, SHOTS, REC, TT), 0.7, 6.0, ((0, 2), (1, 128)))
    delays = with_ends(jax.random.randint(keys[2], (VES, SHOTS), 0, MAXD + 1), jax.random.fold_in(keys[2], 1), 0, MAXD).astype(jnp.int32)
    taps_time = scatter_about(keys[3], (CH, TAPS), TAPS ** -0.5, 2.0, (), jnp.float32)
    taps_shot = scatter_about(keys[4], (CH, TAPS), (TAPS * CH) ** -0.5, 0.5, (), jnp.float32)
    thresh = jnp.clip(jnp.exp(jax.random.uniform(keys[5], (CH,), jnp.float32, math.log(0.02), math.log(0.3))), 0.02, 0.3)
    return {"observed": observed, "estimate": estimate, "delays": delays, "taps_time": taps_time, "taps_shot": taps_shot, "thresh": thresh}


def late_shift(traces, shift_by):
    padded = jnp.pad(traces, ((0, 0), (0, 0), (MAXD, MAXD)))

    def single(trace, shift_amount):
        return lax.dynamic_slice_in_dim(trace, (MAXD - shift_amount).astype(jnp.int32), TT, 1)

    return jax.vmap(single)(padded, shift_by)


def early_shift(traces, shift_by):
    padded = jnp.pad(traces, ((0, 0), (0, 0), (MAXD, MAXD)))

    def single(trace, shift_amount):
        return lax.dynamic_slice_in_dim(trace, (MAXD + shift_amount).astype(jnp.int32), TT, 1)

    return jax.vmap(single)(padded, shift_by)


def along_time(field, taps, shift_sign):
    filter_reach = 3 * TIME_SPACING
    length = field.shape[3]
    padded = jnp.pad(field, ((0, 0), (0, 0), (0, 0), (filter_reach, filter_reach)))
    total = jnp.zeros((taps.shape[0],) + field.shape[1:], jnp.float32)
    for tap_index in range(-3, 4):
        start_offset = filter_reach + shift_sign * tap_index * TIME_SPACING
        total = total + taps[:, tap_index + 3][:, None, None, None] * padded[:, :, :, start_offset:start_offset + length]
    return total


def along_shots(field, taps, shift_sign):
    filter_reach = 3 * SHOT_SPACING
    length = field.shape[1]
    padded = jnp.pad(field, ((0, 0), (filter_reach, filter_reach), (0, 0), (0, 0)))
    total = jnp.zeros((taps.shape[0],) + field.shape[1:], jnp.float32)
    for tap_index in range(-3, 4):
        start_offset = filter_reach + shift_sign * tap_index * SHOT_SPACING
        total = total + taps[:, tap_index + 3][:, None, None, None] * padded[:, start_offset:start_offset + length]
    return total


def shrink_filter(plane, taps_time, taps_shot, thresh):
    field = plane.astype(jnp.float32)[None]
    group_time = taps_time.reshape(-1, 4, taps_time.shape[1])
    group_shot = taps_shot.reshape(-1, 4, taps_shot.shape[1])
    group_thresh = thresh.reshape(-1, 4)

    def channel(carry, pieces):
        time_taps, shot_taps, limits = pieces
        forward_pass = along_shots(along_time(field, time_taps, 1), shot_taps, 1)
        bound = limits[:, None, None, None]
        shrunk = forward_pass - jnp.clip(forward_pass, -bound, bound)
        back = along_time(along_shots(shrunk, shot_taps, -1), time_taps, -1)
        return carry + jnp.sum(back, axis=0), None

    total, _ = lax.scan(channel, jnp.zeros(plane.shape, jnp.float32), (group_time, group_shot, group_thresh))
    return total.astype(jnp.bfloat16)


def reference(observed, estimate, delays, taps_time, taps_shot, thresh):
    current = estimate
    for step in range(ITERS):
        blend = jnp.zeros(observed.shape, jnp.float32)
        for vessel_index in range(VES):
            blend = blend + late_shift(current[vessel_index], delays[vessel_index]).astype(jnp.float32)
        resid = observed.astype(jnp.float32) - blend
        updated = []
        for vessel_index in range(VES):
            plane = (current[vessel_index].astype(jnp.float32) + early_shift(resid, delays[vessel_index])).astype(jnp.bfloat16)
            updated.append(shrink_filter(plane, taps_time, taps_shot, thresh))
        current = jnp.stack(updated)
    return current
```

```python
import functools

import jax
import jax.numpy as jnp
import numpy as np
from jax import lax
from jax.experimental import pallas as pl
from jax.experimental.pallas import tpu as pltpu
from jax.sharding import Mesh, PartitionSpec as P

ITERS = 2
TT = 2048
TILES = TT // 128
HALF = TILES // 2
REC = 128
PAIR = 64
BLOCK = 32
CH = 16
TAPS = 7
STEP = 4
ROWS = CH * BLOCK
COLS = 256
HALO = TAPS * BLOCK
WIDE = TT + 128
TILE = 256
UNROLL = 4


def column_tables():
    tap = np.full((2, COLS), -1, np.int32)
    shot = np.full((2, COLS), -1000, np.int32)
    for block in range(2):
        for k in range(TAPS):
            tap[block, k * BLOCK : (k + 1) * BLOCK] = k
            shot[block, k * BLOCK : (k + 1) * BLOCK] = np.arange(BLOCK)
            at = HALO + 4 * k
            tap[block, at : at + 4] = k
            shot[block, at : at + 4] = np.arange(4) + (BLOCK if block == 0 else -4)
    return tap, shot


def filter_matrices(taps_time, taps_shot):
    tap, shot = column_tables()
    offset = shot[:, None, :] - np.arange(BLOCK)[None, :, None] + 3
    time_part = sum(
        jnp.where(tap[:, None, None, :] == k, taps_time[None, :, None, None, k], 0.0) for k in range(TAPS)
    )
    shot_part = sum(
        jnp.where(offset[:, None] == j, taps_shot[None, :, None, None, j], 0.0) for j in range(TAPS)
    )
    forward = (time_part * shot_part).astype(jnp.bfloat16).reshape(2, ROWS, COLS)
    return forward, forward.transpose(0, 2, 1)


def to_messages(half_ref, x_ref, obs_ref, out_ref, wide_ref):
    for j in range(TILES):
        wide_ref[:, j, :] = x_ref[:, 128 * j : 128 * (j + 1)].astype(jnp.float32)
    for j in range(HALF):
        at = pl.multiple_of((half_ref[0] * HALF + j) * 128, 128)
        wide_ref[:, TILES + j, :] = obs_ref[:, pl.ds(at, 128)].astype(jnp.float32)
    out_ref[...] = wide_ref[...].astype(jnp.bfloat16)


def from_messages(in_ref, out_ref, wide_ref):
    wide_ref[...] = in_ref[...].astype(jnp.float32)
    for j in range(TILES):
        out_ref[:, 128 * j : 128 * (j + 1)] = wide_ref[:, j, :].astype(jnp.bfloat16)


def pack(current, observed, vessel):
    step = 32
    return pl.pallas_call(
        to_messages,
        out_shape=jax.ShapeDtypeStruct((REC, TILES + HALF, 128), jnp.bfloat16),
        grid_spec=pltpu.PrefetchScalarGridSpec(
            num_scalar_prefetch=1,
            grid=(REC // step,),
            in_specs=[
                pl.BlockSpec((step, TT), lambda i, _: (i, 0)),
                pl.BlockSpec((step, TT), lambda i, _: (i, 0)),
            ],
            out_specs=pl.BlockSpec((step, TILES + HALF, 128), lambda i, _: (i, 0, 0)),
            scratch_shapes=[pltpu.VMEM((step, TILES + HALF, 128), jnp.float32)],
        ),
        name="pack",
    )(vessel, current, observed)


def unpack(messages):
    step = 32
    return pl.pallas_call(
        from_messages,
        out_shape=jax.ShapeDtypeStruct((REC, TT), jnp.bfloat16),
        grid=(REC // step,),
        in_specs=[pl.BlockSpec((step, TILES, 128), lambda i: (i, 0, 0))],
        out_specs=pl.BlockSpec((step, TT), lambda i: (i, 0)),
        scratch_shapes=[pltpu.VMEM((step, TILES, 128), jnp.float32)],
        name="unpack",
    )(messages)


def late(x, delay, slot, lane):
    part, whole = delay & 127, delay >> 7
    slot[8:24, :] = pltpu.roll(x, part, 1)
    near = slot[pl.ds(8 - whole, 16), :]
    far = slot[pl.ds(7 - whole, 16), :]
    return jnp.where(lane >= part, near, far)


def early(x, delay, slot, lane):
    part, whole = delay & 127, delay >> 7
    slot[0:16, :] = pltpu.roll(x, (128 - part) & 127, 1)
    near = slot[pl.ds(whole, 16), :]
    far = slot[pl.ds(whole + 1, 16), :]
    return jnp.where(lane < 128 - part, near, far)


def deblend_kernel(
    delays_ref, thresh_ref, recv_ref, fwd_ref, bwd_ref, out_ref,
    traces, observed, planes, wide, columns, halo, shrunk, spread, *slots
):
    lane = lax.broadcasted_iota(jnp.int32, (TILES, 128), 1)
    row = lax.broadcasted_iota(jnp.int32, (8, TT), 0)

    traces[...] = recv_ref[:, :TILES, :].astype(jnp.float32)
    observed[:, :HALF, :] = recv_ref[:PAIR, TILES:, :].astype(jnp.float32)
    observed[:, HALF:, :] = recv_ref[PAIR:, TILES:, :].astype(jnp.float32)
    for slot in slots:
        slot[...] = jnp.zeros_like(slot)
    wide[:, TT:] = jnp.zeros((PAIR, 128), jnp.float32)
    spread[:, :, TT:] = jnp.zeros((2, COLS, 128), jnp.float32)
    halo[...] = jnp.zeros_like(halo)

    def one_iteration(_, carry):
        def blend_some(group, carry):
            for u in range(UNROLL):
                shot = group * UNROLL + u
                first, second = delays_ref[shot], delays_ref[PAIR + shot]
                mine = slots[4 * u : 4 * u + 4]
                a, b = traces[shot], traces[PAIR + shot]
                resid = observed[shot] - (late(a, first, mine[0], lane) + late(b, second, mine[1], lane))
                planes[0, shot] = a + early(resid, first, mine[2], lane)
                planes[1, shot] = b + early(resid, second, mine[3], lane)
            return carry

        lax.fori_loop(0, PAIR // UNROLL, blend_some, 0)

        def one_vessel(vessel, carry):
            for j in range(TILES):
                wide[:, 128 * j : 128 * (j + 1)] = planes[vessel, :, j, :]
            for g in range(PAIR // 16):
                rows = wide[16 * g : 16 * g + 16, :]
                block, inner = g // 2, 16 * (g % 2)
                for k in range(TAPS):
                    moved = rows if k == 3 else pltpu.roll(rows, (STEP * (3 - k)) % WIDE, 1)
                    moved = moved[:, :TT]
                    columns[block, k * BLOCK + inner : k * BLOCK + inner + 16, :] = moved.astype(jnp.bfloat16)
                    if g == 2:
                        halo[0, 4 * k : 4 * k + 4, :] = moved[0:4]
                    if g == 1:
                        halo[1, 4 * k : 4 * k + 4, :] = moved[12:16]
            columns[:, HALO:, :] = halo[...].astype(jnp.bfloat16)

            def one_tile(n, carry):
                at = pl.ds(pl.multiple_of(n * TILE, TILE), TILE)
                for block in range(2):
                    piece = columns[block, :, at]
                    for c4 in range(CH // 4):
                        y = jnp.dot(
                            fwd_ref[block, 128 * c4 : 128 * (c4 + 1), :], piece,
                            preferred_element_type=jnp.float32,
                        )
                        for c in range(4):
                            limit = thresh_ref[4 * c4 + c]
                            part = y[BLOCK * c : BLOCK * (c + 1)]
                            z = part - jnp.clip(part, -limit, limit)
                            start = 128 * c4 + BLOCK * c
                            shrunk[block, start : start + BLOCK, :] = z.astype(jnp.bfloat16)
                    spread[block, :, at] = jnp.dot(
                        bwd_ref[block], shrunk[block], preferred_element_type=jnp.float32
                    )
                return carry

            lax.fori_loop(0, TT // TILE, one_tile, 0)

            for block in range(2):
                for g in range(BLOCK // 8):
                    total = None
                    for k in range(TAPS):
                        part = spread[block, k * BLOCK + 8 * g : k * BLOCK + 8 * g + 8, :]
                        if k != 3:
                            part = pltpu.roll(part, (STEP * (k - 3)) % WIDE, 1)
                        part = part[:, :TT]
                        total = part if total is None else total + part
                    edge = 3 if block == 0 else 0
                    if g == edge:
                        even = odd = None
                        for m in range(4):
                            pair = spread[1 - block, HALO + 8 * m : HALO + 8 * m + 8, :]
                            moved = pltpu.roll(pair, (STEP * (2 * m - 3)) % WIDE, 1)[:, :TT]
                            even = moved if even is None else even + moved
                            if m < 3:
                                moved = pltpu.roll(pair, (STEP * (2 * m - 2)) % WIDE, 1)[:, :TT]
                                odd = moved if odd is None else odd + moved
                        if block == 0:
                            total = total + jnp.where(row >= 4, pltpu.roll(even, 4, 0) + odd, 0.0)
                        else:
                            total = total + jnp.where(row < 4, even + pltpu.roll(odd, 4, 0), 0.0)
                    total = total.astype(jnp.bfloat16).astype(jnp.float32)
                    at = pl.ds(vessel * PAIR + block * BLOCK + 8 * g, 8)
                    for j in range(TILES):
                        traces[at, j, :] = total[:, 128 * j : 128 * (j + 1)]
            return carry

        lax.fori_loop(0, 2, one_vessel, 0)
        return carry

    lax.fori_loop(0, ITERS, one_iteration, 0)
    out_ref[...] = traces[...].astype(jnp.bfloat16)


def deblend(delays, thresh, messages, forward, backward):
    vmem = pl.BlockSpec(memory_space=pltpu.VMEM)
    smem = pl.BlockSpec(memory_space=pltpu.SMEM)
    f32 = jnp.float32
    return pl.pallas_call(
        deblend_kernel,
        out_shape=jax.ShapeDtypeStruct((REC, TILES, 128), jnp.bfloat16),
        in_specs=[smem, smem, vmem, vmem, vmem],
        out_specs=vmem,
        scratch_shapes=[
            pltpu.VMEM((REC, TILES, 128), f32),
            pltpu.VMEM((PAIR, TILES, 128), f32),
            pltpu.VMEM((2, PAIR, TILES, 128), f32),
            pltpu.VMEM((PAIR, WIDE), f32),
            pltpu.VMEM((2, COLS, TT), jnp.bfloat16),
            pltpu.VMEM((2, BLOCK, TT), f32),
            pltpu.VMEM((2, ROWS, TILE), jnp.bfloat16),
            pltpu.VMEM((2, COLS, WIDE), f32),
        ]
        + [pltpu.VMEM((24, 128), f32)] * (4 * UNROLL),
        compiler_params=pltpu.CompilerParams(vmem_limit_bytes=40 << 20),
        name="deblend",
    )(delays, thresh, messages, forward, backward)


def per_device(observed, estimate, delays, taps_time, taps_shot, thresh):
    group = ("vessel", "pairs")
    vessel = lax.axis_index("vessel").reshape(1).astype(jnp.int32)
    sent = pack(estimate[0, 0], observed[0], vessel)
    all_delays = lax.all_gather(delays.reshape(1), group, tiled=True)
    messages = lax.all_to_all(sent, group, split_axis=0, concat_axis=0, tiled=True)
    forward, backward = filter_matrices(taps_time, taps_shot)
    result = deblend(all_delays, thresh, messages, forward, backward)
    back = lax.all_to_all(result, group, split_axis=0, concat_axis=0, tiled=True)
    return unpack(back)[None, None]


def solution(mesh):
    split = Mesh(mesh.devices.reshape(2, PAIR, 2), ("vessel", "pairs", "parity"))
    shots = ("pairs", "parity")
    return jax.shard_map(
        per_device,
        mesh=split,
        in_specs=(
            P(shots, None, None),
            P("vessel", shots, None, None),
            P("vessel", shots),
            P(),
            P(),
            P(),
        ),
        out_specs=P("vessel", shots, None, None),
        check_vma=False,
    )
```

```python
import functools

import jax
import jax.numpy as jnp
import numpy as np
from jax import lax
from jax.experimental import pallas as pl
from jax.experimental.pallas import tpu as pltpu
from jax.sharding import Mesh, PartitionSpec as P

ITERS = 2
TT = 2048
TILES = TT // 128
HALF = TILES // 2
REC = 128
PAIR = 64
BLOCK = 32
CH = 16
TAPS = 7
STEP = 4
ROWS = CH * BLOCK
COLS = 256
HALO = TAPS * BLOCK
WIDE = TT + 128
ITEM = TILES + HALF + 2
TILE = 256
UNROLL = 8


def column_tables():
    tap = np.full((2, COLS), -1, np.int32)
    shot = np.full((2, COLS), -1000, np.int32)
    for block in range(2):
        for k in range(TAPS):
            tap[block, k * BLOCK : (k + 1) * BLOCK] = k
            shot[block, k * BLOCK : (k + 1) * BLOCK] = np.arange(BLOCK)
            at = HALO + 4 * k
            tap[block, at : at + 4] = k
            shot[block, at : at + 4] = np.arange(4) + (BLOCK if block == 0 else -4)
    return tap, shot


def filter_matrices(taps_time, taps_shot):
    tap, shot = column_tables()
    offset = shot[:, None, :] - np.arange(BLOCK)[None, :, None] + 3
    time_part = sum(
        jnp.where(tap[:, None, None, :] == k, taps_time[None, :, None, None, k], 0.0) for k in range(TAPS)
    )
    shot_part = sum(
        jnp.where(offset[:, None] == j, taps_shot[None, :, None, None, j], 0.0) for j in range(TAPS)
    )
    forward = (time_part * shot_part).astype(jnp.bfloat16).reshape(2, ROWS, COLS)
    return forward, forward.transpose(0, 2, 1)


def to_messages(half_ref, delay_ref, x_ref, obs_ref, out_ref, wide_ref):
    rows = x_ref.shape[0]
    for j in range(TILES):
        wide_ref[pl.ds(j, rows, stride=ITEM), :] = x_ref[:, 128 * j : 128 * (j + 1)].astype(jnp.float32)
    for j in range(HALF):
        at = pl.multiple_of((half_ref[0] * HALF + j) * 128, 128)
        wide_ref[pl.ds(TILES + j, rows, stride=ITEM), :] = obs_ref[:, pl.ds(at, 128)].astype(jnp.float32)
    delay = jnp.full((rows, 128), delay_ref[0].astype(jnp.float32), jnp.float32)
    for j in range(TILES + HALF, ITEM):
        wide_ref[pl.ds(j, rows, stride=ITEM), :] = delay
    out_ref[...] = wide_ref[...].astype(jnp.bfloat16)


def from_messages(in_ref, out_ref, wide_ref):
    wide_ref[...] = in_ref[...].astype(jnp.float32)
    for j in range(TILES):
        out_ref[:, 128 * j : 128 * (j + 1)] = wide_ref[:, j, :].astype(jnp.bfloat16)


def pack(current, observed, vessel, delay):
    step = 32
    return pl.pallas_call(
        to_messages,
        out_shape=jax.ShapeDtypeStruct((REC * ITEM, 128), jnp.bfloat16),
        grid_spec=pltpu.PrefetchScalarGridSpec(
            num_scalar_prefetch=2,
            grid=(REC // step,),
            in_specs=[
                pl.BlockSpec((step, TT), lambda i, *_: (i, 0)),
                pl.BlockSpec((step, TT), lambda i, *_: (i, 0)),
            ],
            out_specs=pl.BlockSpec((step * ITEM, 128), lambda i, *_: (i, 0)),
            scratch_shapes=[pltpu.VMEM((step * ITEM, 128), jnp.float32)],
        ),
        name="pack",
    )(vessel, delay, current, observed)


def unpack(messages):
    step = 32
    return pl.pallas_call(
        from_messages,
        out_shape=jax.ShapeDtypeStruct((REC, TT), jnp.bfloat16),
        grid=(REC // step,),
        in_specs=[pl.BlockSpec((step, TILES, 128), lambda i: (i, 0, 0))],
        out_specs=pl.BlockSpec((step, TT), lambda i: (i, 0)),
        scratch_shapes=[pltpu.VMEM((step, TILES, 128), jnp.float32)],
        name="unpack",
    )(messages)


def late(x, delay, slot, lane):
    part, whole = delay & 127, delay >> 7
    slot[8:24, :] = pltpu.roll(x, part, 1)
    near = slot[pl.ds(8 - whole, 16), :]
    far = slot[pl.ds(7 - whole, 16), :]
    return jnp.where(lane >= part, near, far)


def early(x, delay, slot, lane):
    part, whole = delay & 127, delay >> 7
    slot[0:16, :] = pltpu.roll(x, (128 - part) & 127, 1)
    near = slot[pl.ds(whole, 16), :]
    far = slot[pl.ds(whole + 1, 16), :]
    return jnp.where(lane < 128 - part, near, far)


def deblend_kernel(
    thresh_ref, recv_ref, fwd_ref, bwd_ref, out_ref,
    arrived, delay_row, delays_ref, arrival, traces, observed, planes, wide, columns, halo, shrunk, spread, *slots
):
    lane = lax.broadcasted_iota(jnp.int32, (TILES, 128), 1)
    row = lax.broadcasted_iota(jnp.int32, (8, TT), 0)

    arrived[...] = recv_ref[...].astype(jnp.float32)
    by_message = arrived[pl.ds(TILES + HALF, REC, stride=ITEM), :].astype(jnp.int32)
    square = lax.broadcasted_iota(jnp.int32, (REC, 128), 0) == lax.broadcasted_iota(jnp.int32, (REC, 128), 1)
    delay_row[...] = jnp.sum(jnp.where(square, by_message, 0), axis=0, keepdims=True)
    fetch = pltpu.make_async_copy(delay_row, delays_ref, arrival)
    fetch.start()

    def sort_out(group, carry):
        for u in range(8):
            at = group * (8 * ITEM) + u * ITEM
            shot = group * 8 + u
            traces[shot] = arrived[pl.ds(at, TILES), :]
            traces[PAIR + shot] = arrived[pl.ds(at + PAIR * ITEM, TILES), :]
            observed[shot, :HALF, :] = arrived[pl.ds(at + TILES, HALF), :]
            observed[shot, HALF:, :] = arrived[pl.ds(at + PAIR * ITEM + TILES, HALF), :]
        return carry

    lax.fori_loop(0, PAIR // 8, sort_out, 0)
    for slot in slots:
        slot[...] = jnp.zeros_like(slot)
    wide[:, TT:] = jnp.zeros((PAIR, 128), jnp.float32)
    spread[:, :, TT:] = jnp.zeros((2, COLS, 128), jnp.float32)
    halo[...] = jnp.zeros_like(halo)
    fetch.wait()

    def one_iteration(_, carry):
        def blend_some(group, carry):
            for u in range(UNROLL):
                shot = group * UNROLL + u
                first, second = delays_ref[0, shot], delays_ref[0, PAIR + shot]
                mine = slots[4 * u : 4 * u + 4]
                a, b = traces[shot], traces[PAIR + shot]
                resid = observed[shot] - (late(a, first, mine[0], lane) + late(b, second, mine[1], lane))
                planes[0, shot] = a + early(resid, first, mine[2], lane)
                planes[1, shot] = b + early(resid, second, mine[3], lane)
            return carry

        lax.fori_loop(0, PAIR // UNROLL, blend_some, 0)

        def one_vessel(vessel, carry):
            for j in range(TILES):
                wide[:, 128 * j : 128 * (j + 1)] = planes[vessel, :, j, :]
            for g in range(PAIR // 16):
                rows = wide[16 * g : 16 * g + 16, :]
                block, inner = g // 2, 16 * (g % 2)
                for k in range(TAPS):
                    moved = rows if k == 3 else pltpu.roll(rows, (STEP * (3 - k)) % WIDE, 1)
                    moved = moved[:, :TT]
                    columns[block, k * BLOCK + inner : k * BLOCK + inner + 16, :] = moved.astype(jnp.bfloat16)
                    if g == 2:
                        halo[0, 4 * k : 4 * k + 4, :] = moved[0:4]
                    if g == 1:
                        halo[1, 4 * k : 4 * k + 4, :] = moved[12:16]
            columns[:, HALO:, :] = halo[...].astype(jnp.bfloat16)

            def one_tile(n, carry):
                at = pl.ds(pl.multiple_of(n * TILE, TILE), TILE)
                for block in range(2):
                    piece = columns[block, :, at]
                    y = jnp.dot(fwd_ref[block], piece, preferred_element_type=jnp.float32)
                    for c in range(CH):
                        limit = thresh_ref[c]
                        part = y[BLOCK * c : BLOCK * (c + 1)]
                        z = part - jnp.clip(part, -limit, limit)
                        shrunk[block, BLOCK * c : BLOCK * (c + 1), :] = z.astype(jnp.bfloat16)
                    spread[block, :, at] = jnp.dot(
                        bwd_ref[block], shrunk[block], preferred_element_type=jnp.float32
                    )
                return carry

            lax.fori_loop(0, TT // TILE, one_tile, 0, unroll=True)

            for block in range(2):
                for g in range(BLOCK // 8):
                    total = None
                    for k in range(TAPS):
                        part = spread[block, k * BLOCK + 8 * g : k * BLOCK + 8 * g + 8, :]
                        if k != 3:
                            part = pltpu.roll(part, (STEP * (k - 3)) % WIDE, 1)
                        part = part[:, :TT]
                        total = part if total is None else total + part
                    edge = 3 if block == 0 else 0
                    if g == edge:
                        even = odd = None
                        for m in range(4):
                            pair = spread[1 - block, HALO + 8 * m : HALO + 8 * m + 8, :]
                            moved = pltpu.roll(pair, (STEP * (2 * m - 3)) % WIDE, 1)[:, :TT]
                            even = moved if even is None else even + moved
                            if m < 3:
                                moved = pltpu.roll(pair, (STEP * (2 * m - 2)) % WIDE, 1)[:, :TT]
                                odd = moved if odd is None else odd + moved
                        if block == 0:
                            total = total + jnp.where(row >= 4, pltpu.roll(even, 4, 0) + odd, 0.0)
                        else:
                            total = total + jnp.where(row < 4, even + pltpu.roll(odd, 4, 0), 0.0)
                    total = total.astype(jnp.bfloat16).astype(jnp.float32)
                    at = pl.ds(vessel * PAIR + block * BLOCK + 8 * g, 8)
                    for j in range(TILES):
                        traces[at, j, :] = total[:, 128 * j : 128 * (j + 1)]
            return carry

        lax.fori_loop(0, 2, one_vessel, 0, unroll=True)
        return carry

    lax.fori_loop(0, ITERS, one_iteration, 0)
    out_ref[...] = traces[...].astype(jnp.bfloat16)


def deblend(thresh, messages, forward, backward):
    vmem = pl.BlockSpec(memory_space=pltpu.VMEM)
    smem = pl.BlockSpec(memory_space=pltpu.SMEM)
    f32 = jnp.float32
    return pl.pallas_call(
        deblend_kernel,
        out_shape=jax.ShapeDtypeStruct((REC, TILES, 128), jnp.bfloat16),
        in_specs=[smem, vmem, vmem, vmem],
        out_specs=vmem,
        scratch_shapes=[
            pltpu.VMEM((REC * ITEM, 128), f32),
            pltpu.VMEM((1, 128), jnp.int32),
            pltpu.SMEM((1, 128), jnp.int32),
            pltpu.SemaphoreType.DMA,
            pltpu.VMEM((REC, TILES, 128), f32),
            pltpu.VMEM((PAIR, TILES, 128), f32),
            pltpu.VMEM((2, PAIR, TILES, 128), f32),
            pltpu.VMEM((PAIR, WIDE), f32),
            pltpu.VMEM((2, COLS, TT), jnp.bfloat16),
            pltpu.VMEM((2, BLOCK, TT), f32),
            pltpu.VMEM((2, ROWS, TILE), jnp.bfloat16),
            pltpu.VMEM((2, COLS, WIDE), f32),
        ]
        + [pltpu.VMEM((24, 128), f32)] * (4 * UNROLL),
        compiler_params=pltpu.CompilerParams(vmem_limit_bytes=40 << 20),
        name="deblend",
    )(thresh, messages, forward, backward)


def per_device(observed, estimate, delays, taps_time, taps_shot, thresh):
    group = ("vessel", "pairs")
    vessel = lax.axis_index("vessel").reshape(1).astype(jnp.int32)
    sent = pack(estimate[0, 0], observed[0], vessel, delays.reshape(1))
    sent = sent.reshape(REC, ITEM // 2, 2, 128)
    messages = lax.all_to_all(sent, group, split_axis=0, concat_axis=0, tiled=True)
    forward, backward = filter_matrices(taps_time, taps_shot)
    result = deblend(thresh, messages.reshape(REC * ITEM, 128), forward, backward)
    back = lax.all_to_all(result, group, split_axis=0, concat_axis=0, tiled=True)
    return unpack(back)[None, None]


def solution(mesh):
    split = Mesh(mesh.devices.reshape(2, PAIR, 2), ("vessel", "pairs", "parity"))
    shots = ("pairs", "parity")
    return jax.shard_map(
        per_device,
        mesh=split,
        in_specs=(
            P(shots, None, None),
            P("vessel", shots, None, None),
            P("vessel", shots),
            P(),
            P(),
            P(),
        ),
        out_specs=P("vessel", shots, None, None),
        check_vma=False,
    )
```

```python
import functools

import jax
import jax.numpy as jnp
from jax import lax
from jax.experimental import pallas as pl
from jax.experimental.pallas import tpu as pltpu
from jax.sharding import Mesh, PartitionSpec as P

ITERS = 2
TT = 2048
TILES = TT // 128
HALF = TILES // 2
REC = 128
PAIR = 64
BLOCK = 32
CH = 16
TAPS = 7
STEP = 4
ROWS = CH * BLOCK
COLS = 256
HALO = TAPS * BLOCK
WIDE = TT + 128
ITEM = TILES + HALF + 2
TILE = 256
PART = 32
UNROLL = 8


def filter_matrices(time_ref, shot_ref, fwd_ref, bwd_ref):
    lane = lax.broadcasted_iota(jnp.int32, (CH, ROWS), 1)
    chosen = jnp.where(lane // BLOCK == lax.broadcasted_iota(jnp.int32, (CH, ROWS), 0), 1.0, 0.0)
    spread_out = functools.partial(
        jnp.dot, precision=lax.Precision.HIGHEST, preferred_element_type=jnp.float32
    )
    time_taps = spread_out(time_ref[...], chosen)
    shot_taps = spread_out(shot_ref[...], chosen)

    def shot_part(shot, shape):
        offset = shot - lax.broadcasted_iota(jnp.int32, shape, 1) % BLOCK + 3
        total = jnp.zeros(shape, jnp.float32)
        for j in range(TAPS):
            total = jnp.where(offset == j, shot_taps[j : j + 1], total)
        return total

    own = shot_part(lax.broadcasted_iota(jnp.int32, (BLOCK, ROWS), 0), (BLOCK, ROWS))
    main = jnp.concatenate([own * time_taps[k : k + 1] for k in range(TAPS)], axis=0)
    row = lax.broadcasted_iota(jnp.int32, (8, ROWS), 0)
    for block in range(2):
        near = shot_part(row % 4 + (BLOCK if block == 0 else -4), (8, ROWS))
        groups = []
        for m in range(4):
            late_tap = time_taps[2 * m + 1 : 2 * m + 2] if m < 3 else jnp.zeros((1, ROWS), jnp.float32)
            groups.append(near * jnp.where(row < 4, time_taps[2 * m : 2 * m + 1], late_tap))
        both = jnp.concatenate([main] + groups, axis=0)
        bwd_ref[block] = both.astype(jnp.bfloat16)
        fwd_ref[block] = both.T.astype(jnp.bfloat16)


def to_messages(
    half_ref, delay_ref, x_hbm, obs_hbm, time_hbm, shot_hbm, out_ref, fwd_ref, bwd_ref,
    x_ref, obs_ref, time_ref, shot_ref, wide_ref, arrivals, taps_arrivals,
):
    taps = [
        pltpu.make_async_copy(time_hbm, time_ref, taps_arrivals.at[0]),
        pltpu.make_async_copy(shot_hbm, shot_ref, taps_arrivals.at[1]),
    ]
    copies = []
    for part in range(REC // PART):
        rows = pl.ds(PART * part, PART)
        columns = pl.ds(pl.multiple_of(half_ref[0] * (TT // 2), TT // 2), TT // 2)
        copies.append(pltpu.make_async_copy(x_hbm.at[rows], x_ref.at[rows], arrivals.at[2 * part]))
        copies.append(pltpu.make_async_copy(obs_hbm.at[rows, columns], obs_ref.at[rows], arrivals.at[2 * part + 1]))
    for copy in taps + copies:
        copy.start()
    for copy in taps:
        copy.wait()
    filter_matrices(time_ref, shot_ref, fwd_ref, bwd_ref)
    delay = jnp.full((PART, 128), delay_ref[0].astype(jnp.float32), jnp.float32)
    for part in range(REC // PART):
        base = part * PART * ITEM
        rows = pl.ds(PART * part, PART)
        copies[2 * part].wait()
        for j in range(TILES):
            wide_ref[pl.ds(base + j, PART, stride=ITEM), :] = x_ref[rows, 128 * j : 128 * (j + 1)].astype(jnp.float32)
        copies[2 * part + 1].wait()
        for j in range(HALF):
            wide_ref[pl.ds(base + TILES + j, PART, stride=ITEM), :] = obs_ref[
                rows, 128 * j : 128 * (j + 1)
            ].astype(jnp.float32)
        for j in range(TILES + HALF, ITEM):
            wide_ref[pl.ds(base + j, PART, stride=ITEM), :] = delay
        done = pl.ds(base, PART * ITEM)
        out_ref[done, :] = wide_ref[done, :].astype(jnp.bfloat16)


def from_messages(in_ref, out_hbm, wide_ref, out_ref, departures):
    copies = []
    for part in range(REC // PART):
        rows = pl.ds(PART * part, PART)
        wide_ref[rows] = in_ref[rows].astype(jnp.float32)
        for j in range(TILES):
            out_ref[rows, 128 * j : 128 * (j + 1)] = wide_ref[rows, j, :].astype(jnp.bfloat16)
        copies.append(pltpu.make_async_copy(out_ref.at[rows], out_hbm.at[rows], departures.at[part]))
        copies[-1].start()
    for copy in copies:
        copy.wait()


def stay(value):
    return pltpu.with_memory_space_constraint(value, pltpu.HBM)


def pack(current, observed, vessel, delay, taps_time, taps_shot):
    vmem = pl.BlockSpec(memory_space=pltpu.VMEM)
    smem = pl.BlockSpec(memory_space=pltpu.SMEM)
    hbm = pl.BlockSpec(memory_space=pltpu.HBM)
    bf16 = jnp.bfloat16
    return pl.pallas_call(
        to_messages,
        out_shape=(
            jax.ShapeDtypeStruct((REC * ITEM, 128), bf16),
            jax.ShapeDtypeStruct((2, ROWS, COLS), bf16),
            jax.ShapeDtypeStruct((2, COLS, ROWS), bf16),
        ),
        in_specs=[smem, smem, hbm, hbm, hbm, hbm],
        out_specs=(vmem, vmem, vmem),
        scratch_shapes=[
            pltpu.VMEM((REC, TT), bf16),
            pltpu.VMEM((REC, TT // 2), bf16),
            pltpu.VMEM((TAPS, CH), jnp.float32),
            pltpu.VMEM((TAPS, CH), jnp.float32),
            pltpu.VMEM((REC * ITEM, 128), jnp.float32),
            pltpu.SemaphoreType.DMA((2 * REC // PART,)),
            pltpu.SemaphoreType.DMA((2,)),
        ],
        compiler_params=pltpu.CompilerParams(vmem_limit_bytes=16 << 20),
        name="pack",
    )(vessel, delay, *(stay(value) for value in (current, observed, taps_time, taps_shot)))


def unpack(messages):
    return pl.pallas_call(
        from_messages,
        out_shape=jax.ShapeDtypeStruct((REC, TT), jnp.bfloat16),
        in_specs=[pl.BlockSpec(memory_space=pltpu.VMEM)],
        out_specs=pl.BlockSpec(memory_space=pltpu.HBM),
        scratch_shapes=[
            pltpu.VMEM((REC, TILES, 128), jnp.float32),
            pltpu.VMEM((REC, TT), jnp.bfloat16),
            pltpu.SemaphoreType.DMA((REC // PART,)),
        ],
        compiler_params=pltpu.CompilerParams(vmem_limit_bytes=16 << 20),
        name="unpack",
    )(messages)


def late(x, delay, slot, lane):
    part, whole = delay & 127, delay >> 7
    slot[8:24, :] = pltpu.roll(x, part, 1)
    near = slot[pl.ds(8 - whole, 16), :]
    far = slot[pl.ds(7 - whole, 16), :]
    return jnp.where(lane >= part, near, far)


def early(x, delay, slot, lane):
    part, whole = delay & 127, delay >> 7
    slot[0:16, :] = pltpu.roll(x, (128 - part) & 127, 1)
    near = slot[pl.ds(whole, 16), :]
    far = slot[pl.ds(whole + 1, 16), :]
    return jnp.where(lane < 128 - part, near, far)


def deblend_kernel(
    thresh_hbm, recv_ref, fwd_ref, bwd_ref, out_ref,
    thresh_ref, arrived, delay_row, delays_ref, arrivals, traces, observed, planes, wide, columns, halo, shrunk, spread, *slots
):
    lane = lax.broadcasted_iota(jnp.int32, (TILES, 128), 1)
    row = lax.broadcasted_iota(jnp.int32, (8, TT), 0)

    limits = pltpu.make_async_copy(thresh_hbm, thresh_ref, arrivals.at[1])
    limits.start()
    arrived[...] = recv_ref[...].astype(jnp.float32)
    by_message = arrived[pl.ds(TILES + HALF, REC, stride=ITEM), :].astype(jnp.int32)
    square = lax.broadcasted_iota(jnp.int32, (REC, 128), 0) == lax.broadcasted_iota(jnp.int32, (REC, 128), 1)
    delay_row[...] = jnp.sum(jnp.where(square, by_message, 0), axis=0, keepdims=True)
    fetch = pltpu.make_async_copy(delay_row, delays_ref, arrivals.at[0])
    fetch.start()

    def sort_out(group, carry):
        for u in range(8):
            at = group * (8 * ITEM) + u * ITEM
            shot = group * 8 + u
            traces[shot] = arrived[pl.ds(at, TILES), :]
            traces[PAIR + shot] = arrived[pl.ds(at + PAIR * ITEM, TILES), :]
            observed[shot, :HALF, :] = arrived[pl.ds(at + TILES, HALF), :]
            observed[shot, HALF:, :] = arrived[pl.ds(at + PAIR * ITEM + TILES, HALF), :]
        return carry

    lax.fori_loop(0, PAIR // 8, sort_out, 0)
    for slot in slots:
        slot[...] = jnp.zeros_like(slot)
    wide[:, TT:] = jnp.zeros((PAIR, 128), jnp.float32)
    spread[:, :, TT:] = jnp.zeros((2, COLS, 128), jnp.float32)
    halo[...] = jnp.zeros_like(halo)
    fetch.wait()
    limits.wait()

    def one_iteration(_, carry):
        def blend_some(group, carry):
            for u in range(UNROLL):
                shot = group * UNROLL + u
                first, second = delays_ref[0, shot], delays_ref[0, PAIR + shot]
                mine = slots[4 * u : 4 * u + 4]
                a, b = traces[shot], traces[PAIR + shot]
                resid = observed[shot] - (late(a, first, mine[0], lane) + late(b, second, mine[1], lane))
                planes[0, shot] = a + early(resid, first, mine[2], lane)
                planes[1, shot] = b + early(resid, second, mine[3], lane)
            return carry

        lax.fori_loop(0, PAIR // UNROLL, blend_some, 0)

        def one_vessel(vessel, carry):
            for j in range(TILES):
                wide[:, 128 * j : 128 * (j + 1)] = planes[vessel, :, j, :]
            for g in range(PAIR // 16):
                rows = wide[16 * g : 16 * g + 16, :]
                block, inner = g // 2, 16 * (g % 2)
                for k in range(TAPS):
                    moved = rows if k == 3 else pltpu.roll(rows, (STEP * (3 - k)) % WIDE, 1)
                    moved = moved[:, :TT]
                    columns[block, k * BLOCK + inner : k * BLOCK + inner + 16, :] = moved.astype(jnp.bfloat16)
                    if g == 2:
                        halo[0, 4 * k : 4 * k + 4, :] = moved[0:4]
                    if g == 1:
                        halo[1, 4 * k : 4 * k + 4, :] = moved[12:16]
            columns[:, HALO:, :] = halo[...].astype(jnp.bfloat16)

            def one_tile(n, carry):
                at = pl.ds(pl.multiple_of(n * TILE, TILE), TILE)
                for block in range(2):
                    piece = columns[block, :, at]
                    y = jnp.dot(fwd_ref[block], piece, preferred_element_type=jnp.float32)
                    for c in range(CH):
                        limit = thresh_ref[c]
                        part = y[BLOCK * c : BLOCK * (c + 1)]
                        z = part - jnp.clip(part, -limit, limit)
                        shrunk[block, BLOCK * c : BLOCK * (c + 1), :] = z.astype(jnp.bfloat16)
                    spread[block, :, at] = jnp.dot(
                        bwd_ref[block], shrunk[block], preferred_element_type=jnp.float32
                    )
                return carry

            lax.fori_loop(0, TT // TILE, one_tile, 0, unroll=True)

            for block in range(2):
                for g in range(BLOCK // 8):
                    total = None
                    for k in range(TAPS):
                        part = spread[block, k * BLOCK + 8 * g : k * BLOCK + 8 * g + 8, :]
                        if k != 3:
                            part = pltpu.roll(part, (STEP * (k - 3)) % WIDE, 1)
                        part = part[:, :TT]
                        total = part if total is None else total + part
                    edge = 3 if block == 0 else 0
                    if g == edge:
                        even = odd = None
                        for m in range(4):
                            pair = spread[1 - block, HALO + 8 * m : HALO + 8 * m + 8, :]
                            moved = pltpu.roll(pair, (STEP * (2 * m - 3)) % WIDE, 1)[:, :TT]
                            even = moved if even is None else even + moved
                            if m < 3:
                                moved = pltpu.roll(pair, (STEP * (2 * m - 2)) % WIDE, 1)[:, :TT]
                                odd = moved if odd is None else odd + moved
                        if block == 0:
                            total = total + jnp.where(row >= 4, pltpu.roll(even, 4, 0) + odd, 0.0)
                        else:
                            total = total + jnp.where(row < 4, even + pltpu.roll(odd, 4, 0), 0.0)
                    total = total.astype(jnp.bfloat16).astype(jnp.float32)
                    at = pl.ds(vessel * PAIR + block * BLOCK + 8 * g, 8)
                    for j in range(TILES):
                        traces[at, j, :] = total[:, 128 * j : 128 * (j + 1)]
            return carry

        lax.fori_loop(0, 2, one_vessel, 0, unroll=True)
        return carry

    lax.fori_loop(0, ITERS, one_iteration, 0)
    out_ref[...] = traces[...].astype(jnp.bfloat16)


def deblend(thresh, messages, forward, backward):
    vmem = pl.BlockSpec(memory_space=pltpu.VMEM)
    hbm = pl.BlockSpec(memory_space=pltpu.HBM)
    f32 = jnp.float32
    return pl.pallas_call(
        deblend_kernel,
        out_shape=jax.ShapeDtypeStruct((REC, TILES, 128), jnp.bfloat16),
        in_specs=[hbm, vmem, vmem, vmem],
        out_specs=vmem,
        scratch_shapes=[
            pltpu.SMEM((CH,), f32),
            pltpu.VMEM((REC * ITEM, 128), f32),
            pltpu.VMEM((1, 128), jnp.int32),
            pltpu.SMEM((1, 128), jnp.int32),
            pltpu.SemaphoreType.DMA((2,)),
            pltpu.VMEM((REC, TILES, 128), f32),
            pltpu.VMEM((PAIR, TILES, 128), f32),
            pltpu.VMEM((2, PAIR, TILES, 128), f32),
            pltpu.VMEM((PAIR, WIDE), f32),
            pltpu.VMEM((2, COLS, TT), jnp.bfloat16),
            pltpu.VMEM((2, BLOCK, TT), f32),
            pltpu.VMEM((2, ROWS, TILE), jnp.bfloat16),
            pltpu.VMEM((2, COLS, WIDE), f32),
        ]
        + [pltpu.VMEM((24, 128), f32)] * (4 * UNROLL),
        compiler_params=pltpu.CompilerParams(vmem_limit_bytes=40 << 20),
        name="deblend",
    )(stay(thresh), messages, forward, backward)


def per_device(observed, estimate, delays, taps_time, taps_shot, thresh):
    group = ("vessel", "pairs")
    vessel = lax.axis_index("vessel").reshape(1).astype(jnp.int32)
    sent, forward, backward = pack(
        estimate[0, 0], observed[0], vessel, delays.reshape(1), taps_time.T, taps_shot.T
    )
    sent = sent.reshape(REC, ITEM // 2, 2, 128)
    messages = lax.all_to_all(sent, group, split_axis=0, concat_axis=0, tiled=True)
    result = deblend(thresh, messages.reshape(REC * ITEM, 128), forward, backward)
    back = lax.all_to_all(result, group, split_axis=0, concat_axis=0, tiled=True)
    return unpack(back)[None, None]


def solution(mesh):
    split = Mesh(mesh.devices.reshape(2, PAIR, 2), ("vessel", "pairs", "parity"))
    shots = ("pairs", "parity")
    return jax.shard_map(
        per_device,
        mesh=split,
        in_specs=(
            P(shots, None, None),
            P("vessel", shots, None, None),
            P("vessel", shots),
            P(),
            P(),
            P(),
        ),
        out_specs=P("vessel", shots, None, None),
        check_vma=False,
    )
```

```python
import functools

import jax
import jax.numpy as jnp
from jax import lax
from jax.experimental import pallas as pl
from jax.experimental.pallas import tpu as pltpu
from jax.sharding import Mesh, PartitionSpec as P

ITERS = 2
TT = 2048
TILES = TT // 128
HALF = TILES // 2
REC = 128
PAIR = 64
BLOCK = 32
CH = 16
TAPS = 7
STEP = 4
ROWS = CH * BLOCK
COLS = 256
HALO = TAPS * BLOCK
WIDE = TT + 128
ITEM = TILES + HALF + 2
TILE = 256
PART = 32
UNROLL = 8


def filter_matrices(time_ref, shot_ref, fwd_ref, bwd_ref):
    lane = lax.broadcasted_iota(jnp.int32, (CH, ROWS), 1)
    chosen = jnp.where(lane // BLOCK == lax.broadcasted_iota(jnp.int32, (CH, ROWS), 0), 1.0, 0.0)
    spread_out = functools.partial(
        jnp.dot, precision=lax.Precision.HIGHEST, preferred_element_type=jnp.float32
    )
    time_taps = spread_out(time_ref[...], chosen)
    shot_taps = spread_out(shot_ref[...], chosen)

    def shot_part(shot, shape):
        offset = shot - lax.broadcasted_iota(jnp.int32, shape, 1) % BLOCK + 3
        total = jnp.zeros(shape, jnp.float32)
        for j in range(TAPS):
            total = jnp.where(offset == j, shot_taps[j : j + 1], total)
        return total

    own = shot_part(lax.broadcasted_iota(jnp.int32, (BLOCK, ROWS), 0), (BLOCK, ROWS))
    main = jnp.concatenate([own * time_taps[k : k + 1] for k in range(TAPS)], axis=0)
    row = lax.broadcasted_iota(jnp.int32, (8, ROWS), 0)
    for block in range(2):
        near = shot_part(row % 4 + (BLOCK if block == 0 else -4), (8, ROWS))
        groups = []
        for m in range(4):
            late_tap = time_taps[2 * m + 1 : 2 * m + 2] if m < 3 else jnp.zeros((1, ROWS), jnp.float32)
            groups.append(near * jnp.where(row < 4, time_taps[2 * m : 2 * m + 1], late_tap))
        both = jnp.concatenate([main] + groups, axis=0)
        bwd_ref[block] = both.astype(jnp.bfloat16)
        fwd_ref[block] = both.T.astype(jnp.bfloat16)


def to_messages(
    half_ref, delay_ref, x_hbm, obs_hbm, time_hbm, shot_hbm, out_ref, fwd_ref, bwd_ref,
    x_ref, obs_ref, time_ref, shot_ref, wide_ref, arrivals, taps_arrivals,
):
    taps = [
        pltpu.make_async_copy(time_hbm, time_ref, taps_arrivals.at[0]),
        pltpu.make_async_copy(shot_hbm, shot_ref, taps_arrivals.at[1]),
    ]
    copies = []
    for part in range(REC // PART):
        rows = pl.ds(PART * part, PART)
        columns = pl.ds(pl.multiple_of(half_ref[0] * (TT // 2), TT // 2), TT // 2)
        copies.append(pltpu.make_async_copy(x_hbm.at[rows], x_ref.at[rows], arrivals.at[2 * part]))
        copies.append(pltpu.make_async_copy(obs_hbm.at[rows, columns], obs_ref.at[rows], arrivals.at[2 * part + 1]))
    for copy in taps + copies:
        copy.start()
    for copy in taps:
        copy.wait()
    filter_matrices(time_ref, shot_ref, fwd_ref, bwd_ref)
    delay = jnp.full((PART, 128), delay_ref[0].astype(jnp.float32), jnp.float32)
    for part in range(REC // PART):
        base = part * PART * ITEM
        rows = pl.ds(PART * part, PART)
        copies[2 * part].wait()
        for j in range(TILES):
            wide_ref[pl.ds(base + j, PART, stride=ITEM), :] = x_ref[rows, 128 * j : 128 * (j + 1)].astype(jnp.float32)
        copies[2 * part + 1].wait()
        for j in range(HALF):
            wide_ref[pl.ds(base + TILES + j, PART, stride=ITEM), :] = obs_ref[
                rows, 128 * j : 128 * (j + 1)
            ].astype(jnp.float32)
        for j in range(TILES + HALF, ITEM):
            wide_ref[pl.ds(base + j, PART, stride=ITEM), :] = delay
        done = pl.ds(base, PART * ITEM)
        out_ref[done, :] = wide_ref[done, :].astype(jnp.bfloat16)


def from_messages(in_ref, out_hbm, wide_ref, out_ref, departures):
    copies = []
    for part in range(REC // PART):
        rows = pl.ds(PART * part, PART)
        wide_ref[rows] = in_ref[rows].astype(jnp.float32)
        for j in range(TILES):
            out_ref[rows, 128 * j : 128 * (j + 1)] = wide_ref[rows, j, :].astype(jnp.bfloat16)
        copies.append(pltpu.make_async_copy(out_ref.at[rows], out_hbm.at[rows], departures.at[part]))
        copies[-1].start()
    for copy in copies:
        copy.wait()


def stay(value):
    return pltpu.with_memory_space_constraint(value, pltpu.HBM)


def pack(current, observed, vessel, delay, taps_time, taps_shot):
    vmem = pl.BlockSpec(memory_space=pltpu.VMEM)
    smem = pl.BlockSpec(memory_space=pltpu.SMEM)
    hbm = pl.BlockSpec(memory_space=pltpu.HBM)
    bf16 = jnp.bfloat16
    return pl.pallas_call(
        to_messages,
        out_shape=(
            jax.ShapeDtypeStruct((REC * ITEM, 128), bf16),
            jax.ShapeDtypeStruct((2, ROWS, COLS), bf16),
            jax.ShapeDtypeStruct((2, COLS, ROWS), bf16),
        ),
        in_specs=[smem, smem, hbm, hbm, hbm, hbm],
        out_specs=(vmem, vmem, vmem),
        scratch_shapes=[
            pltpu.VMEM((REC, TT), bf16),
            pltpu.VMEM((REC, TT // 2), bf16),
            pltpu.VMEM((TAPS, CH), jnp.float32),
            pltpu.VMEM((TAPS, CH), jnp.float32),
            pltpu.VMEM((REC * ITEM, 128), jnp.float32),
            pltpu.SemaphoreType.DMA((2 * REC // PART,)),
            pltpu.SemaphoreType.DMA((2,)),
        ],
        compiler_params=pltpu.CompilerParams(vmem_limit_bytes=16 << 20),
        name="pack",
    )(vessel, delay, *(stay(value) for value in (current, observed, taps_time, taps_shot)))


def unpack(messages):
    return pl.pallas_call(
        from_messages,
        out_shape=jax.ShapeDtypeStruct((REC, TT), jnp.bfloat16),
        in_specs=[pl.BlockSpec(memory_space=pltpu.VMEM)],
        out_specs=pl.BlockSpec(memory_space=pltpu.HBM),
        scratch_shapes=[
            pltpu.VMEM((REC, TILES, 128), jnp.float32),
            pltpu.VMEM((REC, TT), jnp.bfloat16),
            pltpu.SemaphoreType.DMA((REC // PART,)),
        ],
        compiler_params=pltpu.CompilerParams(vmem_limit_bytes=16 << 20),
        name="unpack",
    )(messages)


def late(x, delay, slot, lane):
    part, whole = delay & 127, delay >> 7
    slot[8:24, :] = pltpu.roll(x, part, 1)
    near = slot[pl.ds(8 - whole, 16), :]
    far = slot[pl.ds(7 - whole, 16), :]
    return jnp.where(lane >= part, near, far)


def early(x, delay, slot, lane):
    part, whole = delay & 127, delay >> 7
    slot[0:16, :] = pltpu.roll(x, (128 - part) & 127, 1)
    near = slot[pl.ds(whole, 16), :]
    far = slot[pl.ds(whole + 1, 16), :]
    return jnp.where(lane < 128 - part, near, far)


def deblend_kernel(
    thresh_hbm, recv_ref, fwd_ref, bwd_ref, out_ref,
    thresh_ref, arrived, delay_row, delays_ref, arrivals, traces, observed, planes, wide, columns, halo, shrunk, spread, *slots
):
    lane = lax.broadcasted_iota(jnp.int32, (TILES, 128), 1)
    row = lax.broadcasted_iota(jnp.int32, (8, TT), 0)

    limits = pltpu.make_async_copy(thresh_hbm, thresh_ref, arrivals.at[1])
    limits.start()
    arrived[...] = recv_ref[...].astype(jnp.float32)
    by_message = arrived[pl.ds(TILES + HALF, REC, stride=ITEM), :].astype(jnp.int32)
    square = lax.broadcasted_iota(jnp.int32, (REC, 128), 0) == lax.broadcasted_iota(jnp.int32, (REC, 128), 1)
    delay_row[...] = jnp.sum(jnp.where(square, by_message, 0), axis=0, keepdims=True)
    fetch = pltpu.make_async_copy(delay_row, delays_ref, arrivals.at[0])
    fetch.start()

    def sort_out(group, carry):
        for u in range(8):
            at = group * (8 * ITEM) + u * ITEM
            shot = group * 8 + u
            traces[shot] = arrived[pl.ds(at, TILES), :]
            traces[PAIR + shot] = arrived[pl.ds(at + PAIR * ITEM, TILES), :]
            observed[shot, :HALF, :] = arrived[pl.ds(at + TILES, HALF), :]
            observed[shot, HALF:, :] = arrived[pl.ds(at + PAIR * ITEM + TILES, HALF), :]
        return carry

    lax.fori_loop(0, PAIR // 8, sort_out, 0)
    for slot in slots:
        slot[...] = jnp.zeros_like(slot)
    wide[:, :, TT:] = jnp.zeros((2, PAIR, 128), jnp.float32)
    spread[:, :, :, TT:] = jnp.zeros((2, 2, COLS, 128), jnp.float32)
    halo[...] = jnp.zeros_like(halo)
    fetch.wait()
    limits.wait()

    def blend_some(group):
        for u in range(UNROLL):
            shot = group * UNROLL + u
            first, second = delays_ref[0, shot], delays_ref[0, PAIR + shot]
            at = 4 * (shot % (2 * UNROLL))
            mine = slots[at : at + 4]
            a, b = traces[shot], traces[PAIR + shot]
            resid = observed[shot] - (late(a, first, mine[0], lane) + late(b, second, mine[1], lane))
            planes[0, shot] = a + early(resid, first, mine[2], lane)
            planes[1, shot] = b + early(resid, second, mine[3], lane)

    def shift_rows(vessel, g):
        some = slice(16 * g, 16 * g + 16)
        for j in range(TILES):
            wide[vessel, some, 128 * j : 128 * (j + 1)] = planes[vessel, some, j, :]
        rows = wide[vessel, some, :]
        block, inner = g // 2, 16 * (g % 2)
        for k in range(TAPS):
            moved = rows if k == 3 else pltpu.roll(rows, (STEP * (3 - k)) % WIDE, 1)
            moved = moved[:, :TT]
            columns[vessel, block, k * BLOCK + inner : k * BLOCK + inner + 16, :] = moved.astype(jnp.bfloat16)
            if g == 2:
                halo[vessel, 0, 4 * k : 4 * k + 4, :] = moved[0:4]
            if g == 1:
                halo[vessel, 1, 4 * k : 4 * k + 4, :] = moved[12:16]

    def place_halo(vessel, block):
        columns[vessel, block, HALO:, :] = halo[vessel, block].astype(jnp.bfloat16)

    def filter_tile(vessel, block, n):
        at = slice(n * TILE, (n + 1) * TILE)
        y = jnp.dot(fwd_ref[block], columns[vessel, block, :, at], preferred_element_type=jnp.float32)
        parts = []
        for c in range(CH):
            limit = thresh_ref[c]
            part = y[BLOCK * c : BLOCK * (c + 1)]
            parts.append((part - jnp.clip(part, -limit, limit)).astype(jnp.bfloat16))
        spread[vessel, block, :, at] = jnp.dot(bwd_ref[block], jnp.concatenate(parts, axis=0), preferred_element_type=jnp.float32)

    def gather_rows(vessel, block, g):
        total = None
        for k in range(TAPS):
            part = spread[vessel, block, k * BLOCK + 8 * g : k * BLOCK + 8 * g + 8, :]
            if k != 3:
                part = pltpu.roll(part, (STEP * (k - 3)) % WIDE, 1)
            part = part[:, :TT]
            total = part if total is None else total + part
        edge = 3 if block == 0 else 0
        if g == edge:
            even = odd = None
            for m in range(4):
                pair = spread[vessel, 1 - block, HALO + 8 * m : HALO + 8 * m + 8, :]
                moved = pltpu.roll(pair, (STEP * (2 * m - 3)) % WIDE, 1)[:, :TT]
                even = moved if even is None else even + moved
                if m < 3:
                    moved = pltpu.roll(pair, (STEP * (2 * m - 2)) % WIDE, 1)[:, :TT]
                    odd = moved if odd is None else odd + moved
            if block == 0:
                total = total + jnp.where(row >= 4, pltpu.roll(even, 4, 0) + odd, 0.0)
            else:
                total = total + jnp.where(row < 4, even + pltpu.roll(odd, 4, 0), 0.0)
        total = total.astype(jnp.bfloat16).astype(jnp.float32)
        at = vessel * PAIR + block * BLOCK + 8 * g
        for j in range(TILES):
            traces[at : at + 8, j, :] = total[:, 128 * j : 128 * (j + 1)]

    def blend(*groups):
        return [functools.partial(blend_some, group) for group in groups]

    def shift(vessel, *groups):
        return [functools.partial(shift_rows, vessel, g) for g in groups]

    def join(vessel, block):
        return [functools.partial(place_halo, vessel, block)]

    def gather(vessel, block, *groups):
        return [functools.partial(gather_rows, vessel, block, g) for g in groups]

    def beside(vessel, block, jobs):
        count = TT // TILE
        for n in range(count):
            filter_tile(vessel, block, n)
            for job in jobs[n * len(jobs) // count : (n + 1) * len(jobs) // count]:
                job()

    def one_iteration(_, carry):
        for job in blend(0, 1, 2, 3) + shift(0, 0, 1) + blend(4, 5) + shift(0, 2) + join(0, 0):
            job()
        beside(0, 0, blend(6, 7) + shift(0, 3) + join(0, 1) + shift(1, 0, 1))
        beside(0, 1, shift(1, 2, 3) + join(1, 0) + join(1, 1) + gather(0, 0, 0, 1, 2))
        beside(1, 0, gather(0, 0, 3) + gather(0, 1, 0, 1, 2, 3))
        beside(1, 1, gather(1, 0, 0, 1, 2))
        for job in gather(1, 0, 3) + gather(1, 1, 0, 1, 2, 3):
            job()
        return carry

    lax.fori_loop(0, ITERS, one_iteration, 0)
    out_ref[...] = traces[...].astype(jnp.bfloat16)


def deblend(thresh, messages, forward, backward):
    vmem = pl.BlockSpec(memory_space=pltpu.VMEM)
    hbm = pl.BlockSpec(memory_space=pltpu.HBM)
    f32 = jnp.float32
    return pl.pallas_call(
        deblend_kernel,
        out_shape=jax.ShapeDtypeStruct((REC, TILES, 128), jnp.bfloat16),
        in_specs=[hbm, vmem, vmem, vmem],
        out_specs=vmem,
        scratch_shapes=[
            pltpu.SMEM((CH,), f32),
            pltpu.VMEM((REC * ITEM, 128), f32),
            pltpu.VMEM((1, 128), jnp.int32),
            pltpu.SMEM((1, 128), jnp.int32),
            pltpu.SemaphoreType.DMA((2,)),
            pltpu.VMEM((REC, TILES, 128), f32),
            pltpu.VMEM((PAIR, TILES, 128), f32),
            pltpu.VMEM((2, PAIR, TILES, 128), f32),
            pltpu.VMEM((2, PAIR, WIDE), f32),
            pltpu.VMEM((2, 2, COLS, TT), jnp.bfloat16),
            pltpu.VMEM((2, 2, BLOCK, TT), f32),
            pltpu.VMEM((4, ROWS, TILE), jnp.bfloat16),
            pltpu.VMEM((2, 2, COLS, WIDE), f32),
        ]
        + [pltpu.VMEM((24, 128), f32)] * (8 * UNROLL),
        compiler_params=pltpu.CompilerParams(vmem_limit_bytes=40 << 20),
        name="deblend",
    )(stay(thresh), messages, forward, backward)


def per_device(observed, estimate, delays, taps_time, taps_shot, thresh):
    group = ("vessel", "pairs")
    vessel = lax.axis_index("vessel").reshape(1).astype(jnp.int32)
    sent, forward, backward = pack(
        estimate[0, 0], observed[0], vessel, delays.reshape(1), taps_time.T, taps_shot.T
    )
    sent = sent.reshape(REC, ITEM // 2, 2, 128)
    messages = lax.all_to_all(sent, group, split_axis=0, concat_axis=0, tiled=True)
    result = deblend(thresh, messages.reshape(REC * ITEM, 128), forward, backward)
    back = lax.all_to_all(result, group, split_axis=0, concat_axis=0, tiled=True)
    return unpack(back)[None, None]


def solution(mesh):
    split = Mesh(mesh.devices.reshape(2, PAIR, 2), ("vessel", "pairs", "parity"))
    shots = ("pairs", "parity")
    return jax.shard_map(
        per_device,
        mesh=split,
        in_specs=(
            P(shots, None, None),
            P("vessel", shots, None, None),
            P("vessel", shots),
            P(),
            P(),
            P(),
        ),
        out_specs=P("vessel", shots, None, None),
        check_vma=False,
    )
```

```python
import functools

import jax
import jax.numpy as jnp
from jax import lax
from jax.experimental import pallas as pl
from jax.experimental.pallas import tpu as pltpu
from jax.sharding import Mesh, PartitionSpec as P

ITERS = 2
TT = 2048
TILES = TT // 128
HALF = TILES // 2
REC = 128
PAIR = 64
BLOCK = 32
CH = 16
TAPS = 7
STEP = 4
ROWS = CH * BLOCK
COLS = 256
HALO = TAPS * BLOCK
WIDE = TT + 128
ITEM = TILES + HALF + 2
TILE = 256
PART = 64
UNROLL = 8


def filter_matrices(time_ref, shot_ref, fwd_ref, bwd_ref):
    lane = lax.broadcasted_iota(jnp.int32, (CH, ROWS), 1)
    chosen = jnp.where(lane // BLOCK == lax.broadcasted_iota(jnp.int32, (CH, ROWS), 0), 1.0, 0.0)
    spread_out = functools.partial(
        jnp.dot, precision=lax.Precision.HIGHEST, preferred_element_type=jnp.float32
    )
    time_taps = spread_out(time_ref[...], chosen)
    shot_taps = spread_out(shot_ref[...], chosen)

    def shot_part(shot, shape):
        offset = shot - lax.broadcasted_iota(jnp.int32, shape, 1) % BLOCK + 3
        total = jnp.zeros(shape, jnp.float32)
        for j in range(TAPS):
            total = jnp.where(offset == j, shot_taps[j : j + 1], total)
        return total

    own = shot_part(lax.broadcasted_iota(jnp.int32, (BLOCK, ROWS), 0), (BLOCK, ROWS))
    main = jnp.concatenate([own * time_taps[k : k + 1] for k in range(TAPS)], axis=0)
    row = lax.broadcasted_iota(jnp.int32, (8, ROWS), 0)
    for block in range(2):
        near = shot_part(row % 4 + (BLOCK if block == 0 else -4), (8, ROWS))
        groups = []
        for m in range(4):
            late_tap = time_taps[2 * m + 1 : 2 * m + 2] if m < 3 else jnp.zeros((1, ROWS), jnp.float32)
            groups.append(near * jnp.where(row < 4, time_taps[2 * m : 2 * m + 1], late_tap))
        both = jnp.concatenate([main] + groups, axis=0)
        bwd_ref[block] = both.astype(jnp.bfloat16)
        fwd_ref[block] = both.T.astype(jnp.bfloat16)


def to_messages(
    half_ref, delay_ref, x_hbm, obs_hbm, time_hbm, shot_hbm, out_ref, fwd_ref, bwd_ref,
    x_ref, obs_ref, time_ref, shot_ref, wide_ref, arrivals, taps_arrivals,
):
    taps = [
        pltpu.make_async_copy(time_hbm, time_ref, taps_arrivals.at[0]),
        pltpu.make_async_copy(shot_hbm, shot_ref, taps_arrivals.at[1]),
    ]
    copies = []
    for part in range(REC // PART):
        rows = pl.ds(PART * part, PART)
        columns = pl.ds(pl.multiple_of(half_ref[0] * (TT // 2), TT // 2), TT // 2)
        copies.append(pltpu.make_async_copy(x_hbm.at[rows], x_ref.at[rows], arrivals.at[2 * part]))
        copies.append(pltpu.make_async_copy(obs_hbm.at[rows, columns], obs_ref.at[rows], arrivals.at[2 * part + 1]))
    for copy in taps + copies:
        copy.start()
    for copy in taps:
        copy.wait()
    filter_matrices(time_ref, shot_ref, fwd_ref, bwd_ref)
    delay = jnp.full((PART, 128), delay_ref[0].astype(jnp.float32), jnp.float32)
    for part in range(REC // PART):
        base = part * PART * ITEM
        rows = pl.ds(PART * part, PART)
        copies[2 * part].wait()
        for j in range(TILES):
            wide_ref[pl.ds(base + j, PART, stride=ITEM), :] = x_ref[rows, 128 * j : 128 * (j + 1)].astype(jnp.float32)
        copies[2 * part + 1].wait()
        for j in range(HALF):
            wide_ref[pl.ds(base + TILES + j, PART, stride=ITEM), :] = obs_ref[
                rows, 128 * j : 128 * (j + 1)
            ].astype(jnp.float32)
        for j in range(TILES + HALF, ITEM):
            wide_ref[pl.ds(base + j, PART, stride=ITEM), :] = delay
        done = pl.ds(base, PART * ITEM)
        out_ref[done, :] = wide_ref[done, :].astype(jnp.bfloat16)


def from_messages(in_ref, out_hbm, wide_ref, out_ref, departures):
    copies = []
    for part in range(REC // PART):
        rows = pl.ds(PART * part, PART)
        out_ref[rows, :] = in_ref[rows].reshape(PART, TT)
        copies.append(pltpu.make_async_copy(out_ref.at[rows], out_hbm.at[rows], departures.at[part]))
        copies[-1].start()
    for copy in copies:
        copy.wait()


def stay(value):
    return pltpu.with_memory_space_constraint(value, pltpu.HBM)


def pack(current, observed, vessel, delay, taps_time, taps_shot):
    vmem = pl.BlockSpec(memory_space=pltpu.VMEM)
    smem = pl.BlockSpec(memory_space=pltpu.SMEM)
    hbm = pl.BlockSpec(memory_space=pltpu.HBM)
    bf16 = jnp.bfloat16
    return pl.pallas_call(
        to_messages,
        out_shape=(
            jax.ShapeDtypeStruct((REC * ITEM, 128), bf16),
            jax.ShapeDtypeStruct((2, ROWS, COLS), bf16),
            jax.ShapeDtypeStruct((2, COLS, ROWS), bf16),
        ),
        in_specs=[smem, smem, hbm, hbm, hbm, hbm],
        out_specs=(vmem, vmem, vmem),
        scratch_shapes=[
            pltpu.VMEM((REC, TT), bf16),
            pltpu.VMEM((REC, TT // 2), bf16),
            pltpu.VMEM((TAPS, CH), jnp.float32),
            pltpu.VMEM((TAPS, CH), jnp.float32),
            pltpu.VMEM((REC * ITEM, 128), jnp.float32),
            pltpu.SemaphoreType.DMA((2 * REC // PART,)),
            pltpu.SemaphoreType.DMA((2,)),
        ],
        compiler_params=pltpu.CompilerParams(vmem_limit_bytes=16 << 20),
        name="pack",
    )(vessel, delay, *(stay(value) for value in (current, observed, taps_time, taps_shot)))


def unpack(messages):
    return pl.pallas_call(
        from_messages,
        out_shape=jax.ShapeDtypeStruct((REC, TT), jnp.bfloat16),
        in_specs=[pl.BlockSpec(memory_space=pltpu.VMEM)],
        out_specs=pl.BlockSpec(memory_space=pltpu.HBM),
        scratch_shapes=[
            pltpu.VMEM((REC, TILES, 128), jnp.float32),
            pltpu.VMEM((REC, TT), jnp.bfloat16),
            pltpu.SemaphoreType.DMA((REC // PART,)),
        ],
        compiler_params=pltpu.CompilerParams(vmem_limit_bytes=16 << 20),
        name="unpack",
    )(messages)


def late(x, delay, slot, lane):
    part, whole = delay & 127, delay >> 7
    slot[8:24, :] = pltpu.roll(x, part, 1)
    near = slot[pl.ds(8 - whole, 16), :]
    far = slot[pl.ds(7 - whole, 16), :]
    return jnp.where(lane >= part, near, far)


def early(x, delay, slot, lane):
    part, whole = delay & 127, delay >> 7
    slot[0:16, :] = pltpu.roll(x, (128 - part) & 127, 1)
    near = slot[pl.ds(whole, 16), :]
    far = slot[pl.ds(whole + 1, 16), :]
    return jnp.where(lane < 128 - part, near, far)


def deblend_kernel(
    thresh_hbm, recv_ref, fwd_ref, bwd_ref, out_ref,
    thresh_ref, arrived, delay_row, delays_ref, arrivals, traces, observed, planes, wide, columns, halo, shrunk, spread, *slots
):
    lane = lax.broadcasted_iota(jnp.int32, (TILES, 128), 1)
    row = lax.broadcasted_iota(jnp.int32, (8, TT), 0)

    limits = pltpu.make_async_copy(thresh_hbm, thresh_ref, arrivals.at[1])
    limits.start()
    arrived[...] = recv_ref[...].astype(jnp.float32)
    by_message = arrived[pl.ds(TILES + HALF, REC, stride=ITEM), :].astype(jnp.int32)
    square = lax.broadcasted_iota(jnp.int32, (REC, 128), 0) == lax.broadcasted_iota(jnp.int32, (REC, 128), 1)
    delay_row[...] = jnp.sum(jnp.where(square, by_message, 0), axis=0, keepdims=True)
    fetch = pltpu.make_async_copy(delay_row, delays_ref, arrivals.at[0])
    fetch.start()

    def sort_out(group, carry):
        for u in range(8):
            at = group * (8 * ITEM) + u * ITEM
            shot = group * 8 + u
            traces[shot] = arrived[pl.ds(at, TILES), :]
            traces[PAIR + shot] = arrived[pl.ds(at + PAIR * ITEM, TILES), :]
            observed[shot, :HALF, :] = arrived[pl.ds(at + TILES, HALF), :]
            observed[shot, HALF:, :] = arrived[pl.ds(at + PAIR * ITEM + TILES, HALF), :]
        return carry

    lax.fori_loop(0, PAIR // 8, sort_out, 0)
    for slot in slots:
        slot[...] = jnp.zeros_like(slot)
    wide[:, :, TT:] = jnp.zeros((2, PAIR, 128), jnp.float32)
    spread[:, :, :, TT:] = jnp.zeros((2, 2, COLS, 128), jnp.float32)
    halo[...] = jnp.zeros_like(halo)
    fetch.wait()
    limits.wait()

    def blend_some(group):
        for u in range(UNROLL):
            shot = group * UNROLL + u
            first, second = delays_ref[0, shot], delays_ref[0, PAIR + shot]
            at = 4 * (shot % (2 * UNROLL))
            mine = slots[at : at + 4]
            a, b = traces[shot], traces[PAIR + shot]
            resid = observed[shot] - (late(a, first, mine[0], lane) + late(b, second, mine[1], lane))
            planes[0, shot] = a + early(resid, first, mine[2], lane)
            planes[1, shot] = b + early(resid, second, mine[3], lane)

    def shift_rows(vessel, g):
        some = slice(16 * g, 16 * g + 16)
        wide[vessel, some, :TT] = planes[vessel, some].reshape(16, TT)
        rows = wide[vessel, some, :]
        block, inner = g // 2, 16 * (g % 2)
        for k in range(TAPS):
            moved = rows if k == 3 else pltpu.roll(rows, (STEP * (3 - k)) % WIDE, 1)
            moved = moved[:, :TT]
            columns[vessel, block, k * BLOCK + inner : k * BLOCK + inner + 16, :] = moved.astype(jnp.bfloat16)
            if g == 2:
                halo[vessel, 0, 4 * k : 4 * k + 4, :] = moved[0:4]
            if g == 1:
                halo[vessel, 1, 4 * k : 4 * k + 4, :] = moved[12:16]

    def place_halo(vessel, block):
        columns[vessel, block, HALO:, :] = halo[vessel, block].astype(jnp.bfloat16)

    def filter_tile(vessel, block, n):
        at = slice(n * TILE, (n + 1) * TILE)
        y = jnp.dot(fwd_ref[block], columns[vessel, block, :, at], preferred_element_type=jnp.float32)
        parts = []
        for c in range(CH):
            limit = thresh_ref[c]
            part = y[BLOCK * c : BLOCK * (c + 1)]
            parts.append((part - jnp.clip(part, -limit, limit)).astype(jnp.bfloat16))
        spread[vessel, block, :, at] = jnp.dot(bwd_ref[block], jnp.concatenate(parts, axis=0), preferred_element_type=jnp.float32)

    def gather_rows(vessel, block, g):
        total = None
        for k in range(TAPS):
            part = spread[vessel, block, k * BLOCK + 8 * g : k * BLOCK + 8 * g + 8, :]
            if k != 3:
                part = pltpu.roll(part, (STEP * (k - 3)) % WIDE, 1)
            part = part[:, :TT]
            total = part if total is None else total + part
        edge = 3 if block == 0 else 0
        if g == edge:
            even = odd = None
            for m in range(4):
                pair = spread[vessel, 1 - block, HALO + 8 * m : HALO + 8 * m + 8, :]
                moved = pltpu.roll(pair, (STEP * (2 * m - 3)) % WIDE, 1)[:, :TT]
                even = moved if even is None else even + moved
                if m < 3:
                    moved = pltpu.roll(pair, (STEP * (2 * m - 2)) % WIDE, 1)[:, :TT]
                    odd = moved if odd is None else odd + moved
            if block == 0:
                total = total + jnp.where(row >= 4, pltpu.roll(even, 4, 0) + odd, 0.0)
            else:
                total = total + jnp.where(row < 4, even + pltpu.roll(odd, 4, 0), 0.0)
        total = total.astype(jnp.bfloat16).astype(jnp.float32)
        at = vessel * PAIR + block * BLOCK + 8 * g
        traces[at : at + 8] = total.reshape(8, TILES, 128)

    def blend(*groups):
        return [functools.partial(blend_some, group) for group in groups]

    def shift(vessel, *groups):
        return [functools.partial(shift_rows, vessel, g) for g in groups]

    def join(vessel, block):
        return [functools.partial(place_halo, vessel, block)]

    def gather(vessel, block, *groups):
        return [functools.partial(gather_rows, vessel, block, g) for g in groups]

    def beside(vessel, block, jobs):
        count = TT // TILE
        for n in range(count):
            filter_tile(vessel, block, n)
            for job in jobs[n * len(jobs) // count : (n + 1) * len(jobs) // count]:
                job()

    def one_iteration(_, carry):
        for job in blend(0, 1, 2, 3) + shift(0, 0, 1) + blend(4, 5) + shift(0, 2) + join(0, 0):
            job()
        beside(0, 0, blend(6, 7) + shift(0, 3) + join(0, 1) + shift(1, 0, 1))
        beside(0, 1, shift(1, 2, 3) + join(1, 0) + join(1, 1) + gather(0, 0, 0, 1, 2))
        beside(1, 0, gather(0, 0, 3) + gather(0, 1, 0, 1, 2, 3))
        beside(1, 1, gather(1, 0, 0, 1, 2))
        for job in gather(1, 0, 3) + gather(1, 1, 0, 1, 2, 3):
            job()
        return carry

    lax.fori_loop(0, ITERS, one_iteration, 0)
    out_ref[...] = traces[...].astype(jnp.bfloat16)


def deblend(thresh, messages, forward, backward):
    vmem = pl.BlockSpec(memory_space=pltpu.VMEM)
    hbm = pl.BlockSpec(memory_space=pltpu.HBM)
    f32 = jnp.float32
    return pl.pallas_call(
        deblend_kernel,
        out_shape=jax.ShapeDtypeStruct((REC, TILES, 128), jnp.bfloat16),
        in_specs=[hbm, vmem, vmem, vmem],
        out_specs=vmem,
        scratch_shapes=[
            pltpu.SMEM((CH,), f32),
            pltpu.VMEM((REC * ITEM, 128), f32),
            pltpu.VMEM((1, 128), jnp.int32),
            pltpu.SMEM((1, 128), jnp.int32),
            pltpu.SemaphoreType.DMA((2,)),
            pltpu.VMEM((REC, TILES, 128), f32),
            pltpu.VMEM((PAIR, TILES, 128), f32),
            pltpu.VMEM((2, PAIR, TILES, 128), f32),
            pltpu.VMEM((2, PAIR, WIDE), f32),
            pltpu.VMEM((2, 2, COLS, TT), jnp.bfloat16),
            pltpu.VMEM((2, 2, BLOCK, TT), f32),
            pltpu.VMEM((4, ROWS, TILE), jnp.bfloat16),
            pltpu.VMEM((2, 2, COLS, WIDE), f32),
        ]
        + [pltpu.VMEM((24, 128), f32)] * (8 * UNROLL),
        compiler_params=pltpu.CompilerParams(vmem_limit_bytes=40 << 20),
        name="deblend",
    )(stay(thresh), messages, forward, backward)


def per_device(observed, estimate, delays, taps_time, taps_shot, thresh):
    group = ("vessel", "pairs")
    vessel = lax.axis_index("vessel").reshape(1).astype(jnp.int32)
    sent, forward, backward = pack(
        estimate[0, 0], observed[0], vessel, delays.reshape(1), taps_time.T, taps_shot.T
    )
    sent = sent.reshape(REC, ITEM // 2, 2, 128)
    messages = lax.all_to_all(sent, group, split_axis=0, concat_axis=0, tiled=True)
    result = deblend(thresh, messages.reshape(REC * ITEM, 128), forward, backward)
    back = lax.all_to_all(result, group, split_axis=0, concat_axis=0, tiled=True)
    return unpack(back)[None, None]


def solution(mesh):
    split = Mesh(mesh.devices.reshape(2, PAIR, 2), ("vessel", "pairs", "parity"))
    shots = ("pairs", "parity")
    return jax.shard_map(
        per_device,
        mesh=split,
        in_specs=(
            P(shots, None, None),
            P("vessel", shots, None, None),
            P("vessel", shots),
            P(),
            P(),
            P(),
        ),
        out_specs=P("vessel", shots, None, None),
        check_vma=False,
    )
```

```python
import functools

import jax
import jax.numpy as jnp
from jax import lax
from jax.experimental import pallas as pl
from jax.experimental.pallas import tpu as pltpu
from jax.sharding import Mesh, PartitionSpec as P

ITERS = 2
TT = 2048
TILES = TT // 128
HALF = TILES // 2
REC = 128
PAIR = 64
BLOCK = 32
CH = 16
TAPS = 7
STEP = 4
ROWS = CH * BLOCK
COLS = 256
HALO = TAPS * BLOCK
WIDE = TT + 128
ITEM = TILES + HALF + 2
TILE = 256
PART = 64
UNROLL = 8


def filter_matrices(time_ref, shot_ref, fwd_ref, bwd_ref):
    lane = lax.broadcasted_iota(jnp.int32, (CH, ROWS), 1)
    chosen = jnp.where(lane // BLOCK == lax.broadcasted_iota(jnp.int32, (CH, ROWS), 0), 1.0, 0.0)
    spread_out = functools.partial(
        jnp.dot, precision=lax.Precision.HIGHEST, preferred_element_type=jnp.float32
    )
    time_taps = spread_out(time_ref[...], chosen)
    shot_taps = spread_out(shot_ref[...], chosen)

    def shot_part(shot, shape):
        offset = shot - lax.broadcasted_iota(jnp.int32, shape, 1) % BLOCK + 3
        total = jnp.zeros(shape, jnp.float32)
        for j in range(TAPS):
            total = jnp.where(offset == j, shot_taps[j : j + 1], total)
        return total

    own = shot_part(lax.broadcasted_iota(jnp.int32, (BLOCK, ROWS), 0), (BLOCK, ROWS))
    main = jnp.concatenate([own * time_taps[k : k + 1] for k in range(TAPS)], axis=0)
    row = lax.broadcasted_iota(jnp.int32, (8, ROWS), 0)
    for block in range(2):
        near = shot_part(row % 4 + (BLOCK if block == 0 else -4), (8, ROWS))
        groups = []
        for m in range(4):
            late_tap = time_taps[2 * m + 1 : 2 * m + 2] if m < 3 else jnp.zeros((1, ROWS), jnp.float32)
            groups.append(near * jnp.where(row < 4, time_taps[2 * m : 2 * m + 1], late_tap))
        both = jnp.concatenate([main] + groups, axis=0)
        bwd_ref[block] = both.astype(jnp.bfloat16)
        fwd_ref[block] = both.T.astype(jnp.bfloat16)


def to_messages(
    half_ref, delay_ref, x_hbm, obs_hbm, time_hbm, shot_hbm, out_ref, fwd_ref, bwd_ref,
    x_ref, obs_ref, time_ref, shot_ref, wide_ref, arrivals, taps_arrivals,
):
    taps = [
        pltpu.make_async_copy(time_hbm, time_ref, taps_arrivals.at[0]),
        pltpu.make_async_copy(shot_hbm, shot_ref, taps_arrivals.at[1]),
    ]
    copies = []
    for part in range(REC // PART):
        rows = pl.ds(PART * part, PART)
        columns = pl.ds(pl.multiple_of(half_ref[0] * (TT // 2), TT // 2), TT // 2)
        copies.append(pltpu.make_async_copy(x_hbm.at[rows], x_ref.at[rows], arrivals.at[2 * part]))
        copies.append(pltpu.make_async_copy(obs_hbm.at[rows, columns], obs_ref.at[rows], arrivals.at[2 * part + 1]))
    for copy in taps + copies:
        copy.start()
    for copy in taps:
        copy.wait()
    filter_matrices(time_ref, shot_ref, fwd_ref, bwd_ref)
    delay = jnp.full((PART, 128), delay_ref[0].astype(jnp.float32), jnp.float32)
    for part in range(REC // PART):
        base = part * PART * ITEM
        rows = pl.ds(PART * part, PART)
        copies[2 * part].wait()
        for j in range(TILES):
            wide_ref[pl.ds(base + j, PART, stride=ITEM), :] = x_ref[rows, 128 * j : 128 * (j + 1)].astype(jnp.float32)
        copies[2 * part + 1].wait()
        for j in range(HALF):
            wide_ref[pl.ds(base + TILES + j, PART, stride=ITEM), :] = obs_ref[
                rows, 128 * j : 128 * (j + 1)
            ].astype(jnp.float32)
        for j in range(TILES + HALF, ITEM):
            wide_ref[pl.ds(base + j, PART, stride=ITEM), :] = delay
        done = pl.ds(base, PART * ITEM)
        out_ref[done, :] = wide_ref[done, :].astype(jnp.bfloat16)


def from_messages(in_ref, out_hbm, wide_ref, out_ref, departures):
    copies = []
    for part in range(REC // PART):
        rows = pl.ds(PART * part, PART)
        out_ref[rows, :] = in_ref[rows].reshape(PART, TT)
        copies.append(pltpu.make_async_copy(out_ref.at[rows], out_hbm.at[rows], departures.at[part]))
        copies[-1].start()
    for copy in copies:
        copy.wait()


def stay(value):
    return pltpu.with_memory_space_constraint(value, pltpu.HBM)


def pack(current, observed, vessel, delay, taps_time, taps_shot):
    vmem = pl.BlockSpec(memory_space=pltpu.VMEM)
    smem = pl.BlockSpec(memory_space=pltpu.SMEM)
    hbm = pl.BlockSpec(memory_space=pltpu.HBM)
    bf16 = jnp.bfloat16
    return pl.pallas_call(
        to_messages,
        out_shape=(
            jax.ShapeDtypeStruct((REC * ITEM, 128), bf16),
            jax.ShapeDtypeStruct((2, ROWS, COLS), bf16),
            jax.ShapeDtypeStruct((2, COLS, ROWS), bf16),
        ),
        in_specs=[smem, smem, hbm, hbm, hbm, hbm],
        out_specs=(vmem, vmem, vmem),
        scratch_shapes=[
            pltpu.VMEM((REC, TT), bf16),
            pltpu.VMEM((REC, TT // 2), bf16),
            pltpu.VMEM((TAPS, CH), jnp.float32),
            pltpu.VMEM((TAPS, CH), jnp.float32),
            pltpu.VMEM((REC * ITEM, 128), jnp.float32),
            pltpu.SemaphoreType.DMA((2 * REC // PART,)),
            pltpu.SemaphoreType.DMA((2,)),
        ],
        compiler_params=pltpu.CompilerParams(vmem_limit_bytes=16 << 20),
        name="pack",
    )(vessel, delay, *(stay(value) for value in (current, observed, taps_time, taps_shot)))


def unpack(messages):
    return pl.pallas_call(
        from_messages,
        out_shape=jax.ShapeDtypeStruct((REC, TT), jnp.bfloat16),
        in_specs=[pl.BlockSpec(memory_space=pltpu.VMEM)],
        out_specs=pl.BlockSpec(memory_space=pltpu.HBM),
        scratch_shapes=[
            pltpu.VMEM((REC, TILES, 128), jnp.float32),
            pltpu.VMEM((REC, TT), jnp.bfloat16),
            pltpu.SemaphoreType.DMA((REC // PART,)),
        ],
        compiler_params=pltpu.CompilerParams(vmem_limit_bytes=16 << 20),
        name="unpack",
    )(messages)


def late(x, delay, slot, lane):
    part, whole = delay & 127, delay >> 7
    slot[8:24, :] = pltpu.roll(x, part, 1)
    near = slot[pl.ds(8 - whole, 16), :]
    far = slot[pl.ds(7 - whole, 16), :]
    return jnp.where(lane >= part, near, far)


def early(x, delay, slot, lane):
    part, whole = delay & 127, delay >> 7
    slot[0:16, :] = pltpu.roll(x, (128 - part) & 127, 1)
    near = slot[pl.ds(whole, 16), :]
    far = slot[pl.ds(whole + 1, 16), :]
    return jnp.where(lane < 128 - part, near, far)


def deblend_kernel(
    thresh_hbm, recv_ref, fwd_ref, bwd_ref, out_ref,
    thresh_ref, arrived, delay_row, delays_ref, arrivals, traces, observed, wide, columns, halo, shrunk, spread, *slots
):
    lane = lax.broadcasted_iota(jnp.int32, (TILES, 128), 1)
    row = lax.broadcasted_iota(jnp.int32, (8, TT), 0)

    limits = pltpu.make_async_copy(thresh_hbm, thresh_ref, arrivals.at[1])
    limits.start()
    arrived[...] = recv_ref[...].astype(jnp.float32)
    by_message = arrived[pl.ds(TILES + HALF, REC, stride=ITEM), :].astype(jnp.int32)
    square = lax.broadcasted_iota(jnp.int32, (REC, 128), 0) == lax.broadcasted_iota(jnp.int32, (REC, 128), 1)
    delay_row[...] = jnp.sum(jnp.where(square, by_message, 0), axis=0, keepdims=True)
    fetch = pltpu.make_async_copy(delay_row, delays_ref, arrivals.at[0])
    fetch.start()

    def sort_out(group, carry):
        for u in range(8):
            at = group * (8 * ITEM) + u * ITEM
            shot = group * 8 + u
            traces[shot] = arrived[pl.ds(at, TILES), :]
            traces[PAIR + shot] = arrived[pl.ds(at + PAIR * ITEM, TILES), :]
            observed[shot, :HALF, :] = arrived[pl.ds(at + TILES, HALF), :]
            observed[shot, HALF:, :] = arrived[pl.ds(at + PAIR * ITEM + TILES, HALF), :]
        return carry

    lax.fori_loop(0, PAIR // 8, sort_out, 0)
    for slot in slots:
        slot[...] = jnp.zeros_like(slot)
    wide[:, :, TT:] = jnp.zeros((2, PAIR, 128), jnp.float32)
    spread[:, :, :, TT:] = jnp.zeros((2, 2, COLS, 128), jnp.float32)
    halo[...] = jnp.zeros_like(halo)
    fetch.wait()
    limits.wait()

    def blend_some(group):
        made = ([], [])
        for u in range(UNROLL):
            shot = group * UNROLL + u
            first, second = delays_ref[0, shot], delays_ref[0, PAIR + shot]
            at = 4 * (shot % (2 * UNROLL))
            mine = slots[at : at + 4]
            a, b = traces[shot], traces[PAIR + shot]
            resid = observed[shot] - (late(a, first, mine[0], lane) + late(b, second, mine[1], lane))
            made[0].append(a + early(resid, first, mine[2], lane))
            made[1].append(b + early(resid, second, mine[3], lane))
        some = slice(group * UNROLL, (group + 1) * UNROLL)
        for vessel in range(2):
            wide[vessel, some, :TT] = jnp.stack(made[vessel]).reshape(UNROLL, TT)

    def shift_rows(vessel, g):
        some = slice(16 * g, 16 * g + 16)
        rows = wide[vessel, some, :]
        block, inner = g // 2, 16 * (g % 2)
        for k in range(TAPS):
            moved = rows if k == 3 else pltpu.roll(rows, (STEP * (3 - k)) % WIDE, 1)
            moved = moved[:, :TT]
            columns[vessel, block, k * BLOCK + inner : k * BLOCK + inner + 16, :] = moved.astype(jnp.bfloat16)
            if g == 2:
                halo[vessel, 0, 4 * k : 4 * k + 4, :] = moved[0:4]
            if g == 1:
                halo[vessel, 1, 4 * k : 4 * k + 4, :] = moved[12:16]

    def place_halo(vessel, block):
        columns[vessel, block, HALO:, :] = halo[vessel, block].astype(jnp.bfloat16)

    def filter_tile(vessel, block, n):
        at = slice(n * TILE, (n + 1) * TILE)
        y = jnp.dot(fwd_ref[block], columns[vessel, block, :, at], preferred_element_type=jnp.float32)
        parts = []
        for c in range(CH):
            limit = thresh_ref[c]
            part = y[BLOCK * c : BLOCK * (c + 1)]
            parts.append((part - jnp.clip(part, -limit, limit)).astype(jnp.bfloat16))
        spread[vessel, block, :, at] = jnp.dot(bwd_ref[block], jnp.concatenate(parts, axis=0), preferred_element_type=jnp.float32)

    def gather_rows(vessel, block, g):
        total = None
        for k in range(TAPS):
            part = spread[vessel, block, k * BLOCK + 8 * g : k * BLOCK + 8 * g + 8, :]
            if k != 3:
                part = pltpu.roll(part, (STEP * (k - 3)) % WIDE, 1)
            part = part[:, :TT]
            total = part if total is None else total + part
        edge = 3 if block == 0 else 0
        if g == edge:
            even = odd = None
            for m in range(4):
                pair = spread[vessel, 1 - block, HALO + 8 * m : HALO + 8 * m + 8, :]
                moved = pltpu.roll(pair, (STEP * (2 * m - 3)) % WIDE, 1)[:, :TT]
                even = moved if even is None else even + moved
                if m < 3:
                    moved = pltpu.roll(pair, (STEP * (2 * m - 2)) % WIDE, 1)[:, :TT]
                    odd = moved if odd is None else odd + moved
            if block == 0:
                total = total + jnp.where(row >= 4, pltpu.roll(even, 4, 0) + odd, 0.0)
            else:
                total = total + jnp.where(row < 4, even + pltpu.roll(odd, 4, 0), 0.0)
        total = total.astype(jnp.bfloat16).astype(jnp.float32)
        at = vessel * PAIR + block * BLOCK + 8 * g
        traces[at : at + 8] = total.reshape(8, TILES, 128)

    def blend(*groups):
        return [functools.partial(blend_some, group) for group in groups]

    def shift(vessel, *groups):
        return [functools.partial(shift_rows, vessel, g) for g in groups]

    def join(vessel, block):
        return [functools.partial(place_halo, vessel, block)]

    def gather(vessel, block, *groups):
        return [functools.partial(gather_rows, vessel, block, g) for g in groups]

    def beside(vessel, block, jobs):
        count = TT // TILE
        for n in range(count):
            filter_tile(vessel, block, n)
            for job in jobs[n * len(jobs) // count : (n + 1) * len(jobs) // count]:
                job()

    def one_iteration(_, carry):
        for job in blend(0, 1, 2, 3) + shift(0, 0, 1) + blend(4, 5) + shift(0, 2) + join(0, 0):
            job()
        beside(0, 0, blend(6, 7) + shift(0, 3) + join(0, 1) + shift(1, 0, 1))
        beside(0, 1, shift(1, 2, 3) + join(1, 0) + join(1, 1) + gather(0, 0, 0, 1, 2))
        beside(1, 0, gather(0, 0, 3) + gather(0, 1, 0, 1, 2, 3))
        beside(1, 1, gather(1, 0, 0, 1, 2))
        for job in gather(1, 0, 3) + gather(1, 1, 0, 1, 2, 3):
            job()
        return carry

    lax.fori_loop(0, ITERS, one_iteration, 0)
    out_ref[...] = traces[...].astype(jnp.bfloat16)


def deblend(thresh, messages, forward, backward):
    vmem = pl.BlockSpec(memory_space=pltpu.VMEM)
    hbm = pl.BlockSpec(memory_space=pltpu.HBM)
    f32 = jnp.float32
    return pl.pallas_call(
        deblend_kernel,
        out_shape=jax.ShapeDtypeStruct((REC, TILES, 128), jnp.bfloat16),
        in_specs=[hbm, vmem, vmem, vmem],
        out_specs=vmem,
        scratch_shapes=[
            pltpu.SMEM((CH,), f32),
            pltpu.VMEM((REC * ITEM, 128), f32),
            pltpu.VMEM((1, 128), jnp.int32),
            pltpu.SMEM((1, 128), jnp.int32),
            pltpu.SemaphoreType.DMA((2,)),
            pltpu.VMEM((REC, TILES, 128), f32),
            pltpu.VMEM((PAIR, TILES, 128), f32),
            pltpu.VMEM((2, PAIR, WIDE), f32),
            pltpu.VMEM((2, 2, COLS, TT), jnp.bfloat16),
            pltpu.VMEM((2, 2, BLOCK, TT), f32),
            pltpu.VMEM((4, ROWS, TILE), jnp.bfloat16),
            pltpu.VMEM((2, 2, COLS, WIDE), f32),
        ]
        + [pltpu.VMEM((24, 128), f32)] * (8 * UNROLL),
        compiler_params=pltpu.CompilerParams(vmem_limit_bytes=40 << 20),
        name="deblend",
    )(stay(thresh), messages, forward, backward)


def per_device(observed, estimate, delays, taps_time, taps_shot, thresh):
    group = ("vessel", "pairs")
    vessel = lax.axis_index("vessel").reshape(1).astype(jnp.int32)
    sent, forward, backward = pack(
        estimate[0, 0], observed[0], vessel, delays.reshape(1), taps_time.T, taps_shot.T
    )
    sent = sent.reshape(REC, ITEM // 2, 2, 128)
    messages = lax.all_to_all(sent, group, split_axis=0, concat_axis=0, tiled=True)
    result = deblend(thresh, messages.reshape(REC * ITEM, 128), forward, backward)
    back = lax.all_to_all(result, group, split_axis=0, concat_axis=0, tiled=True)
    return unpack(back)[None, None]


def solution(mesh):
    split = Mesh(mesh.devices.reshape(2, PAIR, 2), ("vessel", "pairs", "parity"))
    shots = ("pairs", "parity")
    return jax.shard_map(
        per_device,
        mesh=split,
        in_specs=(
            P(shots, None, None),
            P("vessel", shots, None, None),
            P("vessel", shots),
            P(),
            P(),
            P(),
        ),
        out_specs=P("vessel", shots, None, None),
        check_vma=False,
    )
```
